32 devices in a mesh: dp: 4 (over z), expert: 8 (over y, x, core).
Axes of the slice: x: 2, y: 2, z: 4, core: 2. Of those that a mesh axis runs over, the one named last changes fastest.
Arguments:
- tokens: bfloat16 [4, 2048, 2048], P('dp', 'expert'), may hold values from -8 to 8
- cotangent: bfloat16 [4, 2048, 2048], P('dp', 'expert'), may hold values from -8 to 8
- slot_rows: int32 [4, 8, 8, 32], P('dp', 'expert'), may hold values from 0 to 255, as said below
- slot_count: int32 [4, 8, 8], P('dp', 'expert'), may hold values from 8 to 32, as said below
- slot_weight: float32 [4, 8, 8, 32], P('dp', 'expert'), may hold values from 0.1 to 1
- w_in: bfloat16 [8, 2, 2048, 512], P('expert'), may hold values from -5 to 5
- w_out: bfloat16 [8, 512, 2048], P('expert'), may hold values from -5 to 5
- momentum_in: float32 [8, 2, 2048, 512], P('expert', None, 'dp'), may hold values from -6 to 6
- momentum_out: float32 [8, 512, 2048], P('expert', None, 'dp'), may hold values from -6 to 6
Outputs:
- token_grad: bfloat16 [4, 2048, 2048], P('dp', 'expert')
- w_in_new: bfloat16 [8, 2, 2048, 512], P('expert')
- w_out_new: bfloat16 [8, 512, 2048], P('expert')
- momentum_in_new: float32 [8, 2, 2048, 512], P('expert', None, 'dp')
- momentum_out_new: float32 [8, 512, 2048], P('expert', None, 'dp')
The draws below stay inside these ranges and needn't reach their ends.
Inputs may be any that keep to these rules, and one draw needn't show every extreme that they name: `slot_rows`: entries index the source's 256 tokens; the 32 entries of one source and expert are distinct. Slots c < slot_count are used. In every replica some expert receives 32 rows from every source.
All inputs are finite; a program needn't handle non-finite values.
Results may differ from the reference program's by a relative error of at most 0.0064.
Values may be sent and summed in bfloat16 or wider, within the bound.
No kernel may reach another device: no remote copies, remote signals or barrier semaphores. Data moves between devices by JAX's collectives and lax.ppermute only.
A program may use at most 128 MiB of HBM per device.

```python
import math
import jax
import jax.numpy as jnp
from jax import lax

D = 2048
FF = 512
LEVELS = 2
TOK_DEV = 256
CAP = 32
EXPERTS = 8
TOKENS = 2048
ROWS = 256
N_DP = 4
N_EXPERT = 8


def feature_draw(key, rows_total, feature_width):
    key_scale = jax.random.fold_in(key, 0)
    key_common = jax.random.fold_in(key, 1)
    key_noise = jax.random.fold_in(key, 2)
    key_own = jax.random.fold_in(key, 4)
    key_replica = jax.random.fold_in(key, 5)
    column_scale = jnp.exp(jax.random.uniform(key_scale, (feature_width,), jnp.float32, 0.0, math.log(10.0)))
    column_scale = column_scale / jnp.sqrt(jnp.mean(column_scale * column_scale))
    shared = jax.random.normal(key_common, (1, 1, feature_width), jnp.float32)
    own = jax.random.normal(key_own, (N_DP, 1, feature_width), jnp.float32)
    replica_scale = jnp.exp(jax.random.uniform(key_replica, (N_DP, 1, 1), jnp.float32, math.log(0.6), math.log(1.6)))
    noise_part = jax.random.normal(key_noise, (N_DP, rows_total, feature_width), jnp.float32)
    result = replica_scale * (0.5 * (shared + 0.8 * own) + noise_part) * column_scale
    return jnp.clip(result, -8.0, 8.0)


def draw_tokens(key, part):
    return feature_draw(jax.random.fold_in(key, 11), TOKENS, D).astype(jnp.bfloat16)


def draw_cotangent(key, part):
    return feature_draw(jax.random.fold_in(key, 23), TOKENS, D).astype(jnp.bfloat16)


def draw_slot_rows(key, part):
    scores = jax.random.randint(jax.random.fold_in(key, 31), (N_DP, N_EXPERT, EXPERTS, TOK_DEV), 0, (1 << 30) // TOK_DEV)
    scores = scores * TOK_DEV + lax.broadcasted_iota(jnp.int32, scores.shape, 3)
    chosen = jnp.argsort(scores, axis=-1, stable=True)[..., :CAP]
    return chosen.astype(jnp.int32)


def draw_slot_count(key, part):
    key_counts, key_full = jax.random.split(jax.random.fold_in(key, 47))
    lowest = max(1, CAP // 4)
    counts = jax.random.randint(key_counts, (N_DP, N_EXPERT, EXPERTS), lowest, CAP + 1)
    full_expert = jax.random.randint(key_full, (N_DP, 1, 1), 0, EXPERTS)
    expert_ids = lax.broadcasted_iota(jnp.int32, counts.shape, 2)
    return jnp.where(expert_ids == full_expert, CAP, counts).astype(jnp.int32)


def shard_levels(rng, dims, cuts, smallest, top_value):
    level, own = 1.0, jax.random.fold_in(rng, 6)
    for axis_at, shards_of in cuts:
        draws = jnp.exp(jax.random.uniform(jax.random.fold_in(own, axis_at), (shards_of,), jnp.float32, smallest / len(cuts), top_value / len(cuts)))
        level = level * jnp.repeat(draws, dims[axis_at] // shards_of).reshape([-1 if axis == axis_at else 1 for axis in range(len(dims))])
    return level


def normal_values(rng, shape, width, most, cuts=(), kind=jnp.bfloat16):
    values = jax.random.normal(rng, shape, jnp.float32) * width
    if len(cuts) > 0:
        values = shard_levels(rng, shape, cuts, -0.22, 0.18) * values
    return jnp.clip(values, min=-most, max=most).astype(kind)


def setup_inputs(seed: int = 0) -> dict:
    key_of = jax.random.split(jax.random.key(seed), 10)
    tokens = draw_tokens(jax.random.fold_in(key_of[9], 71), 0)
    cotangent = draw_cotangent(jax.random.fold_in(key_of[9], 71), 0)
    slot_rows = draw_slot_rows(jax.random.fold_in(key_of[9], 71), 0)
    slot_count = draw_slot_count(jax.random.fold_in(key_of[9], 71), 0)
    slot_weight = jnp.clip(jnp.exp(math.log(1.0) - 2.3025851 * jax.random.uniform(key_of[4], (N_DP, N_EXPERT, EXPERTS, CAP), jnp.float32) ** shard_levels(key_of[4], (N_DP, N_EXPERT, EXPERTS, CAP), ((0, 4), (1, 8)), -0.2, 0.2)), 0.1, 1.0)
    w_in = normal_values(key_of[5], (EXPERTS, 2, D, FF), 1.0, 5.0, ((0, 8),))
    w_out = normal_values(key_of[6], (EXPERTS, FF, D), 1.0, 5.0, ((0, 8),))
    momentum_in = normal_values(key_of[7], (EXPERTS, 2, D, FF), 1.0, 6.0, ((0, 8), (2, 4)), jnp.float32)
    momentum_out = normal_values(key_of[8], (EXPERTS, FF, D), 1.0, 6.0, ((0, 8), (2, 4)), jnp.float32)
    return {"tokens": tokens, "cotangent": cotangent, "slot_rows": slot_rows, "slot_count": slot_count, "slot_weight": slot_weight, "w_in": w_in, "w_out": w_out, "momentum_in": momentum_in, "momentum_out": momentum_out}


adasum_eps = 1e-6
momentum_coef = 0.9
learn_rate = 0.1


def expert_backward(routed_rows, cotan_rows, w_gate, w_up, w_down):
    scale_in = routed_rows.shape[1] ** -0.5
    scale_out = w_gate.shape[1] ** -0.5
    gate_proj = jnp.dot(routed_rows, w_gate, preferred_element_type=jnp.float32) * scale_in
    up_proj = jnp.dot(routed_rows, w_up, preferred_element_type=jnp.float32) * scale_in
    sigmoid_gate = jax.nn.sigmoid(gate_proj)
    activated = gate_proj * sigmoid_gate
    hidden_act = (activated * up_proj).astype(jnp.bfloat16)
    grad_down = jnp.dot(hidden_act.T, cotan_rows, preferred_element_type=jnp.float32) * scale_out
    hidden_grad = jnp.dot(cotan_rows, w_down.T, preferred_element_type=jnp.float32) * scale_out
    gate_grad = (hidden_grad * up_proj * sigmoid_gate * (1.0 + gate_proj * (1.0 - sigmoid_gate))).astype(jnp.bfloat16)
    up_grad = (hidden_grad * activated).astype(jnp.bfloat16)
    grad_gate = jnp.dot(routed_rows.T, gate_grad, preferred_element_type=jnp.float32) * scale_in
    grad_up = jnp.dot(routed_rows.T, up_grad, preferred_element_type=jnp.float32) * scale_in
    rows_back = (jnp.dot(gate_grad, w_gate.T, preferred_element_type=jnp.float32)
                 + jnp.dot(up_grad, w_up.T, preferred_element_type=jnp.float32)) * scale_in
    return jnp.stack([grad_gate, grad_up]), grad_down, rows_back.astype(jnp.bfloat16)


def inner_terms(former, latter):
    return jnp.sum(former[0] * latter[0]) + jnp.sum(former[1] * latter[1])


def adasum(former, latter):
    cross_term = inner_terms(former, latter)
    coef_former = 1.0 - cross_term / (2.0 * (inner_terms(former, former) + adasum_eps))
    coef_latter = 1.0 - cross_term / (2.0 * (inner_terms(latter, latter) + adasum_eps))
    return (coef_former * former[0] + coef_latter * latter[0], coef_former * former[1] + coef_latter * latter[1])


def reference(tokens, cotangent, slot_rows, slot_count, slot_weight, w_in, w_out, momentum_in, momentum_out):
    is_valid = (jnp.arange(CAP, dtype=jnp.int32)[None, None, None, :] < slot_count[:, :, :, None]).astype(jnp.float32)
    slot_scale = slot_weight * is_valid
    offsets = (jnp.arange(N_EXPERT, dtype=jnp.int32) * TOK_DEV)[None, :, None, None]
    token_index = (slot_rows + offsets).astype(jnp.int32)

    def per_expert(token_grad, expert_id):
        chosen = lax.dynamic_index_in_dim(token_index, expert_id, 2, keepdims=False).reshape(N_DP, ROWS)
        scales = lax.dynamic_index_in_dim(slot_scale, expert_id, 2, keepdims=False).reshape(N_DP, ROWS)
        w_pair = lax.dynamic_index_in_dim(w_in, expert_id, 0, keepdims=False)
        w_down = lax.dynamic_index_in_dim(w_out, expert_id, 0, keepdims=False)
        vectors = []
        for replica in range(N_DP):
            routed_rows = tokens[replica][chosen[replica]]
            cotan_rows = (cotangent[replica][chosen[replica]].astype(jnp.float32) * scales[replica][:, None]).astype(jnp.bfloat16)
            grad_wide, grad_narrow, rows_back = expert_backward(routed_rows, cotan_rows, w_pair[0], w_pair[1], w_down)
            token_grad = token_grad.at[replica, chosen[replica]].add(rows_back.astype(jnp.float32))
            vectors.append((grad_wide, grad_narrow))
        for level_bit in range(LEVELS - 1, -1, -1):
            stride = 2 ** level_bit
            vectors = [adasum(vectors[lower_id], vectors[lower_id + stride]) for lower_id in range(stride)]
        combined = vectors[0]
        momentum_wide = momentum_coef * lax.dynamic_index_in_dim(momentum_in, expert_id, 0, keepdims=False) + combined[0]
        momentum_narrow = momentum_coef * lax.dynamic_index_in_dim(momentum_out, expert_id, 0, keepdims=False) + combined[1]
        new_wide = (w_pair.astype(jnp.float32) - learn_rate * momentum_wide).astype(jnp.bfloat16)
        new_narrow = (w_down.astype(jnp.float32) - learn_rate * momentum_narrow).astype(jnp.bfloat16)
        return token_grad, (new_wide, new_narrow, momentum_wide, momentum_narrow)

    initial = jnp.zeros((N_DP, TOKENS, D), jnp.float32)
    token_grad, stacked = lax.scan(per_expert, initial, jnp.arange(EXPERTS, dtype=jnp.int32))
    return (token_grad.astype(jnp.bfloat16), stacked[0], stacked[1], stacked[2], stacked[3])
```

```python
import functools

import jax
import jax.numpy as jnp
from jax import lax
from jax.experimental import pallas as pl
from jax.experimental.pallas import tpu as pltpu
from jax.sharding import PartitionSpec as P

adasum_eps = 1e-06
momentum_coef = 0.9
learn_rate = 0.1


LANES = 128


def contract(lhs_operand, rhs_operand, left_dim, right_dim):
    return lax.dot_general(
        lhs_operand,
        rhs_operand,
        (((left_dim,), (right_dim,)), ((), ())),
        preferred_element_type=jnp.float32,
    )


def vmem_spec():
    return pl.BlockSpec(memory_space=pltpu.VMEM)


def smem_spec():
    return pl.BlockSpec(memory_space=pltpu.SMEM)


def dispatch_kernel(position, index_ref, limit_ref, gain_ref, tokens_ref, cotan_ref, sent_ref, *rest):
    slice_refs, (select_ref, scale_ref, piece_ref) = rest[:-3], rest[-3:]
    experts, capacity = index_ref.shape
    token_count, model_width = tokens_ref.shape
    replicas = piece_ref.shape[0]
    quarter = model_width // replicas
    row_id = lax.broadcasted_iota(jnp.int32, (capacity, capacity), 0)
    col_id = lax.broadcasted_iota(jnp.int32, (capacity, capacity), 1)
    diagonal = row_id == col_id
    slot_id = lax.broadcasted_iota(jnp.int32, (capacity, 1), 0)
    lane_id = lax.broadcasted_iota(jnp.int32, (capacity, token_count), 1)
    for expert in range(experts):
        rows = slice(expert * capacity, (expert + 1) * capacity)
        wanted = jnp.sum(jnp.where(diagonal, index_ref[expert : expert + 1, :].astype(jnp.float32), 0.0), axis=1, keepdims=True)
        gain = jnp.sum(jnp.where(diagonal, gain_ref[expert : expert + 1, :], 0.0), axis=1, keepdims=True)
        scale_ref[rows, :] = jnp.where(slot_id < limit_ref[0, expert], gain, 0.0)
        select_ref[rows, :] = (lane_id == wanted.astype(jnp.int32)).astype(jnp.float32).astype(jnp.bfloat16)
    select = select_ref[...]
    scale = scale_ref[...]
    for part in range(replicas):
        columns = slice(part * quarter, (part + 1) * quarter)
        rows_x = contract(select, tokens_ref[:, columns], 1, 0).astype(jnp.bfloat16)
        rows_g = (contract(select, cotan_ref[:, columns], 1, 0) * scale).astype(jnp.bfloat16)
        sent_ref[:, columns] = rows_x
        sent_ref[:, model_width + part * quarter : model_width + (part + 1) * quarter] = rows_g
        piece_ref[part, :, :quarter] = rows_x
        piece_ref[part, :, quarter:] = rows_g
    for hop, slice_ref in enumerate(slice_refs, start=1):
        slice_ref[...] = piece_ref[(position[0] + hop) % replicas]


def dispatch(position, slot_index, slot_limit, slot_gain, tokens, cotan, replicas):
    experts, capacity = slot_index.shape
    token_count, model_width = tokens.shape
    rows = experts * capacity
    quarter = model_width // replicas
    return pl.pallas_call(
        dispatch_kernel,
        in_specs=[smem_spec(), vmem_spec(), smem_spec(), vmem_spec(), vmem_spec(), vmem_spec()],
        out_specs=[vmem_spec()] * replicas,
        out_shape=[jax.ShapeDtypeStruct((rows, 2 * model_width), jnp.bfloat16)]
        + [jax.ShapeDtypeStruct((rows, 2 * quarter), jnp.bfloat16)] * (replicas - 1),
        scratch_shapes=[
            pltpu.VMEM((rows, token_count), jnp.bfloat16),
            pltpu.VMEM((rows, 1), jnp.float32),
            pltpu.VMEM((replicas, rows, 2 * quarter), jnp.bfloat16),
        ],
        name="dispatch",
    )(position, slot_index, slot_limit, slot_gain, tokens, cotan)


def slot_slice(peer_ref, slot, start, width):
    block = peer_ref[:, slot, :, start : start + width]
    return block.reshape(block.shape[0] * block.shape[1], width)


def gram_kernel(replicas, scale_in, scale_out, position, own_ref, peer_ref, *rest):
    wide_refs, hidden_refs, gram_ref = rest[:replicas], rest[replicas : 2 * replicas], rest[-1]
    quarter = own_ref.shape[1] // 2

    def side(slot, start):
        if slot == 0:
            return own_ref[:, start : start + quarter]
        return slot_slice(peer_ref, slot - 1, start, quarter)

    for former in range(replicas):
        for latter in range(former, replicas):
            rows_pair = contract(side(former, 0), side(latter, 0), 1, 1)
            wide_pair = contract(wide_refs[former][...], wide_refs[latter][...], 1, 1)
            cotan_pair = contract(side(former, quarter), side(latter, quarter), 1, 1)
            hidden_pair = contract(hidden_refs[former][...], hidden_refs[latter][...], 1, 1)
            terms = rows_pair * wide_pair * (scale_in * scale_in) + cotan_pair * hidden_pair * (scale_out * scale_out)
            total = jnp.full((1, LANES), jnp.sum(terms), jnp.float32)
            row_former = (position[0] + replicas - former) % replicas
            row_latter = (position[0] + replicas - latter) % replicas
            gram_ref[pl.ds(row_former * replicas + row_latter, 1), :] = total
            gram_ref[pl.ds(row_latter * replicas + row_former, 1), :] = total


def gram_share(position, own, peers, wides, hiddens, scale_in, scale_out):
    replicas = len(wides)
    return pl.pallas_call(
        functools.partial(gram_kernel, replicas, scale_in, scale_out),
        in_specs=[smem_spec()] + [vmem_spec()] * (2 + 2 * replicas),
        out_specs=vmem_spec(),
        out_shape=jax.ShapeDtypeStruct((replicas * replicas, LANES), jnp.float32),
        name="gram",
    )(position, own, peers, *wides, *hiddens)


def tree_weights(gram, replicas):
    inner = [[gram[a * replicas + b : a * replicas + b + 1, :] for b in range(replicas)] for a in range(replicas)]
    weights = [{replica: None} for replica in range(replicas)]
    stride = replicas // 2
    while stride:
        for lower in range(stride):
            cross = inner[lower][lower + stride]
            norm_former = jnp.maximum(inner[lower][lower], 0.0)
            norm_latter = jnp.maximum(inner[lower + stride][lower + stride], 0.0)
            bound = jnp.sqrt(norm_former) * jnp.sqrt(norm_latter)
            cross = jnp.clip(cross, -bound, bound)
            former = 1.0 - cross / (2.0 * (norm_former + adasum_eps))
            latter = 1.0 - cross / (2.0 * (norm_latter + adasum_eps))
            joined = {}
            for side, factor in ((lower, former), (lower + stride, latter)):
                for replica, weight in weights[side].items():
                    joined[replica] = factor if weight is None else factor * weight
            weights[lower] = joined
            rows = [former * inner[lower][b] + latter * inner[lower + stride][b] for b in range(2 * stride)]
            inner[lower] = rows
            for a in range(2 * stride):
                if a != lower:
                    inner[a][lower] = former * inner[a][lower] + latter * inner[a][lower + stride]
            inner[lower][lower] = former * rows[lower] + latter * rows[lower + stride]
        stride //= 2
    return [weights[0][replica] for replica in range(replicas)]


def step_weights(position, gram_refs, weight_ref):
    replicas = len(gram_refs)
    total = gram_refs[0][...]
    for gram_ref in gram_refs[1:]:
        total = total + gram_ref[...]
    for replica, weight in enumerate(tree_weights(total, replicas)):
        weight_ref[replica : replica + 1, :] = weight

    def weight_of(slot, width):
        row = weight_ref[pl.ds((position[0] + replicas - slot) % replicas, 1), :]
        return jnp.concatenate([row] * (width // LANES), axis=1)

    return weight_of


def finish_step(combined, momentum, weight):
    momentum_new = momentum_coef * momentum + combined
    return momentum_new, (weight.astype(jnp.float32) - learn_rate * momentum_new).astype(jnp.bfloat16)


def narrow_step_kernel(replicas, scale, position, *refs):
    gram_refs = refs[:replicas]
    own_ref, peer_ref = refs[replicas : replicas + 2]
    hidden_refs = refs[replicas + 2 : 2 * replicas + 2]
    momentum_ref, weight_ref, momentum_out_ref, weight_out_ref, mix_ref = refs[2 * replicas + 2 :]
    quarter = own_ref.shape[1] // 2
    weight_of = step_weights(position, gram_refs, mix_ref)
    combined = 0.0
    for slot in range(replicas):
        cotan = own_ref[:, quarter:] if slot == 0 else slot_slice(peer_ref, slot - 1, quarter, quarter)
        combined = combined + contract(hidden_refs[slot][...], cotan, 0, 0) * (weight_of(slot, quarter) * scale)
    momentum_new, weight_new = finish_step(combined, momentum_ref[0], weight_ref[0])
    momentum_out_ref[0] = momentum_new
    weight_out_ref[...] = weight_new


def wide_step_kernel(replicas, scale, position, *refs):
    gram_refs = refs[:replicas]
    own_ref, peer_ref = refs[replicas : replicas + 2]
    wide_refs = refs[replicas + 2 : 2 * replicas + 2]
    momentum_ref, weight_ref, momentum_out_ref, weight_out_ref, mix_ref = refs[2 * replicas + 2 :]
    quarter = own_ref.shape[1] // 2
    hidden = wide_refs[0].shape[1]
    weight_of = step_weights(position, gram_refs, mix_ref)
    combined = 0.0
    for slot in range(replicas):
        rows = own_ref[:, :quarter] if slot == 0 else slot_slice(peer_ref, slot - 1, 0, quarter)
        combined = combined + contract(rows, wide_refs[slot][...], 0, 0) * (weight_of(slot, hidden) * scale)
    momentum_new, weight_new = finish_step(combined, momentum_ref[0, 0], weight_ref[0, 0])
    momentum_out_ref[0, 0] = momentum_new
    weight_out_ref[0] = weight_new


def whole_block(array):
    return pl.BlockSpec(array.shape, lambda part, position: (0,) * array.ndim)


def narrow_step(position, grams, own, peers, hiddens, momentum, weight, scale):
    replicas = len(grams)
    hidden, quarter = momentum.shape[1:]
    inputs = [*grams, own, peers, *hiddens]
    return pl.pallas_call(
        functools.partial(narrow_step_kernel, replicas, scale),
        grid_spec=pltpu.PrefetchScalarGridSpec(
            num_scalar_prefetch=1,
            grid=(1,),
            in_specs=[whole_block(array) for array in inputs]
            + [
                whole_block(momentum),
                pl.BlockSpec((1, hidden, quarter), lambda part, position: (0, 0, position[0])),
            ],
            out_specs=[
                whole_block(momentum),
                pl.BlockSpec((hidden, quarter), lambda part, position: (0, 0)),
            ],
            scratch_shapes=[pltpu.VMEM((8, LANES), jnp.float32)],
        ),
        out_shape=[
            jax.ShapeDtypeStruct(momentum.shape, jnp.float32),
            jax.ShapeDtypeStruct((hidden, quarter), jnp.bfloat16),
        ],
        name="narrow_step",
    )(position, *inputs, momentum, weight)


def wide_step(position, grams, own, peers, wides, momentum, weight, scale):
    replicas = len(grams)
    quarter, hidden = momentum.shape[2:]
    inputs = [*grams, own, peers]
    return pl.pallas_call(
        functools.partial(wide_step_kernel, replicas, scale),
        grid_spec=pltpu.PrefetchScalarGridSpec(
            num_scalar_prefetch=1,
            grid=(2,),
            in_specs=[whole_block(array) for array in inputs]
            + [pl.BlockSpec((array.shape[0], hidden), lambda part, position: (0, part)) for array in wides]
            + [
                pl.BlockSpec((1, 1, quarter, hidden), lambda part, position: (0, part, 0, 0)),
                pl.BlockSpec((1, 1, quarter, hidden), lambda part, position: (0, part, position[0], 0)),
            ],
            out_specs=[
                pl.BlockSpec((1, 1, quarter, hidden), lambda part, position: (0, part, 0, 0)),
                pl.BlockSpec((1, quarter, hidden), lambda part, position: (part, 0, 0)),
            ],
            scratch_shapes=[pltpu.VMEM((8, LANES), jnp.float32)],
        ),
        out_shape=[
            jax.ShapeDtypeStruct(momentum.shape, jnp.float32),
            jax.ShapeDtypeStruct((2, quarter, hidden), jnp.bfloat16),
        ],
        name="wide_step",
    )(position, *inputs, *wides, momentum, weight)


def relay(value):
    replicas = lax.axis_size("dp")
    rightward, leftward = [], []
    right, left = value, value
    for hop in range(1, replicas):
        right = lax.ppermute(right, "dp", [(i, i + 1) for i in range(hop - 1, replicas - 1)])
        left = lax.ppermute(left, "dp", [(i, i - 1) for i in range(1, replicas - hop + 1)])
        rightward.append(right)
        leftward.append(left)
    return rightward, leftward


def pick_slot(position, rightward, leftward, hop):
    return jnp.where(position >= hop, rightward[hop - 1], leftward[len(leftward) - hop])


def shards(
    tokens, cotangent, slot_rows, slot_count, slot_weight, w_in, w_out, momentum_in, momentum_out
):
    expert_axis = lax.axis_size("expert")
    replicas = lax.axis_size("dp")
    position = lax.axis_index("dp")
    position_arg = position.astype(jnp.int32).reshape(1)
    token_count, model_width = tokens.shape[1:]
    capacity = slot_rows.shape[-1]
    hidden = w_out.shape[1]
    quarter = model_width // replicas
    rows = expert_axis * capacity
    scale_in = model_width ** (-0.5)
    scale_out = hidden ** (-0.5)

    sent, *slices = dispatch(
        position_arg, slot_rows[0, 0], slot_count[0], slot_weight[0, 0], tokens[0], cotangent[0], replicas
    )
    moved = [
        lax.ppermute(piece, "dp", [(i, (i + hop) % replicas) for i in range(replicas)])
        for hop, piece in enumerate(slices, start=1)
    ]
    routed = lax.all_to_all(
        sent.reshape(expert_axis, capacity, 2 * model_width), "expert", split_axis=0, concat_axis=0, tiled=True
    ).reshape(rows, 2 * model_width)
    routed_rows = routed[:, :model_width]
    routed_cotan = routed[:, model_width:]

    gate_proj = jnp.dot(routed_rows, w_in[0, 0], preferred_element_type=jnp.float32) * scale_in
    up_proj = jnp.dot(routed_rows, w_in[0, 1], preferred_element_type=jnp.float32) * scale_in
    sigmoid_gate = jax.nn.sigmoid(gate_proj)
    activated = gate_proj * sigmoid_gate
    hidden_act = (activated * up_proj).astype(jnp.bfloat16)
    hidden_grad = contract(routed_cotan, w_out[0], 1, 1) * scale_out
    gate_grad = (
        hidden_grad * up_proj * sigmoid_gate * (1.0 + gate_proj * (1.0 - sigmoid_gate))
    ).astype(jnp.bfloat16)
    up_grad = (hidden_grad * activated).astype(jnp.bfloat16)
    wide_grad = jnp.concatenate([gate_grad, up_grad], axis=1)

    hidden_moves = relay(hidden_act)
    wide_moves = relay(wide_grad)
    own = jnp.concatenate(
        [
            lax.dynamic_slice_in_dim(routed, position * quarter, quarter, 1),
            lax.dynamic_slice_in_dim(routed, model_width + position * quarter, quarter, 1),
        ],
        axis=1,
    )
    peers = lax.all_to_all(
        jnp.stack([piece.reshape(expert_axis, capacity, 2 * quarter) for piece in moved], axis=1),
        "expert",
        split_axis=0,
        concat_axis=0,
        tiled=True,
    )

    rows_back = (
        (contract(gate_grad, w_in[0, 0], 1, 1) + contract(up_grad, w_in[0, 1], 1, 1)) * scale_in
    ).astype(jnp.bfloat16)
    returned = lax.all_to_all(
        rows_back.reshape(expert_axis, capacity, model_width), "expert", split_axis=0, concat_axis=0, tiled=True
    )
    flat_index = slot_rows.reshape(-1)
    one_hot = (
        flat_index[None, :] == lax.broadcasted_iota(jnp.int32, (token_count, flat_index.shape[0]), 0)
    ).astype(jnp.bfloat16)
    token_grad = jnp.dot(
        one_hot, returned.reshape(-1, model_width), preferred_element_type=jnp.float32
    ).astype(jnp.bfloat16)[None]

    hiddens = [hidden_act] + [pick_slot(position, *hidden_moves, hop) for hop in range(1, replicas)]
    wides = [wide_grad] + [pick_slot(position, *wide_moves, hop) for hop in range(1, replicas)]
    gram = gram_share(position_arg, own, peers, wides, hiddens, scale_in, scale_out)
    grams = [gram] + [
        lax.ppermute(gram, "dp", [(i, (i + hop) % replicas) for i in range(replicas)])
        for hop in range(1, replicas)
    ]
    momentum_narrow, block_narrow = narrow_step(
        position_arg, grams, own, peers, hiddens, momentum_out, w_out, scale_out
    )
    momentum_wide, block_wide = wide_step(
        position_arg, grams, own, peers, wides, momentum_in, w_in, scale_in
    )
    narrow_moves = relay(block_narrow)
    wide_block_moves = relay(block_wide)
    new_narrow = jnp.zeros(w_out.shape, jnp.bfloat16)
    new_wide = jnp.zeros(w_in.shape, jnp.bfloat16)
    for hop in (0, *range(1, replicas)):
        start = (position + replicas - hop) % replicas * quarter
        narrow = block_narrow if hop == 0 else pick_slot(position, *narrow_moves, hop)
        wide = block_wide if hop == 0 else pick_slot(position, *wide_block_moves, hop)
        new_narrow = lax.dynamic_update_slice(new_narrow, narrow[None], (0, 0, start))
        new_wide = lax.dynamic_update_slice(new_wide, wide[None], (0, 0, start, 0))
    return (token_grad, new_wide, new_narrow, momentum_wide, momentum_narrow)


def solution(mesh):
    return jax.shard_map(
        shards,
        mesh=mesh,
        in_specs=(
            P("dp", "expert", None),
            P("dp", "expert", None),
            P("dp", "expert", None, None),
            P("dp", "expert", None),
            P("dp", "expert", None, None),
            P("expert", None, None, None),
            P("expert", None, None),
            P("expert", None, "dp", None),
            P("expert", None, "dp"),
        ),
        out_specs=(
            P("dp", "expert", None),
            P("expert", None, None, None),
            P("expert", None, None),
            P("expert", None, "dp", None),
            P("expert", None, "dp"),
        ),
        check_vma=False,
    )
```

```python
import functools

import jax
import jax.numpy as jnp
from jax import lax
from jax.experimental import pallas as pl
from jax.experimental.pallas import tpu as pltpu
from jax.sharding import PartitionSpec as P


adasum_eps = 1e-06
momentum_coef = 0.9
learn_rate = 0.1


LANES = 128


def contract(lhs_operand, rhs_operand, left_dim, right_dim):
    return lax.dot_general(
        lhs_operand,
        rhs_operand,
        (((left_dim,), (right_dim,)), ((), ())),
        preferred_element_type=jnp.float32,
    )


def vmem_spec():
    return pl.BlockSpec(memory_space=pltpu.VMEM)


def smem_spec():
    return pl.BlockSpec(memory_space=pltpu.SMEM)


def dispatch_kernel(position, index_ref, limit_ref, gain_ref, tokens_ref, cotan_ref, sent_ref, *rest):
    slice_refs, (select_ref, scale_ref, piece_ref) = rest[:-3], rest[-3:]
    experts, capacity = index_ref.shape
    token_count, model_width = tokens_ref.shape
    replicas = piece_ref.shape[0]
    quarter = model_width // replicas
    row_id = lax.broadcasted_iota(jnp.int32, (capacity, capacity), 0)
    col_id = lax.broadcasted_iota(jnp.int32, (capacity, capacity), 1)
    diagonal = row_id == col_id
    slot_id = lax.broadcasted_iota(jnp.int32, (capacity, 1), 0)
    lane_id = lax.broadcasted_iota(jnp.int32, (capacity, token_count), 1)
    for expert in range(experts):
        rows = slice(expert * capacity, (expert + 1) * capacity)
        wanted = jnp.sum(jnp.where(diagonal, index_ref[expert : expert + 1, :].astype(jnp.float32), 0.0), axis=1, keepdims=True)
        gain = jnp.sum(jnp.where(diagonal, gain_ref[expert : expert + 1, :], 0.0), axis=1, keepdims=True)
        scale_ref[rows, :] = jnp.where(slot_id < limit_ref[0, expert], gain, 0.0)
        select_ref[rows, :] = (lane_id == wanted.astype(jnp.int32)).astype(jnp.float32).astype(jnp.bfloat16)
    select = select_ref[...]
    scale = scale_ref[...]
    for part in range(replicas):
        columns = slice(part * quarter, (part + 1) * quarter)
        rows_x = contract(select, tokens_ref[:, columns], 1, 0).astype(jnp.bfloat16)
        rows_g = (contract(select, cotan_ref[:, columns], 1, 0) * scale).astype(jnp.bfloat16)
        sent_ref[:, columns] = rows_x
        sent_ref[:, model_width + part * quarter : model_width + (part + 1) * quarter] = rows_g
        piece_ref[part, :, :quarter] = rows_x
        piece_ref[part, :, quarter:] = rows_g
    for hop, slice_ref in enumerate(slice_refs, start=1):
        slice_ref[...] = piece_ref[(position[0] + hop) % replicas]


def dispatch(position, slot_index, slot_limit, slot_gain, tokens, cotan, replicas):
    experts, capacity = slot_index.shape
    token_count, model_width = tokens.shape
    rows = experts * capacity
    quarter = model_width // replicas
    return pl.pallas_call(
        dispatch_kernel,
        in_specs=[smem_spec(), vmem_spec(), smem_spec(), vmem_spec(), vmem_spec(), vmem_spec()],
        out_specs=[vmem_spec()] * replicas,
        out_shape=[jax.ShapeDtypeStruct((rows, 2 * model_width), jnp.bfloat16)]
        + [jax.ShapeDtypeStruct((rows, 2 * quarter), jnp.bfloat16)] * (replicas - 1),
        scratch_shapes=[
            pltpu.VMEM((rows, token_count), jnp.bfloat16),
            pltpu.VMEM((rows, 1), jnp.float32),
            pltpu.VMEM((replicas, rows, 2 * quarter), jnp.bfloat16),
        ],
        name="dispatch",
    )(position, slot_index, slot_limit, slot_gain, tokens, cotan)


def slot_slice(peer_ref, slot, start, width):
    block = peer_ref[:, slot, :, start : start + width]
    return block.reshape(block.shape[0] * block.shape[1], width)


def hbm_spec():
    return pl.BlockSpec(memory_space=pltpu.HBM)


def replica_pairs(replicas):
    return [(former, latter) for former in range(replicas) for latter in range(former, replicas)]


def inner_rows(gradient_ref, pairs):
    height, width = gradient_ref.shape[1:]
    chunk = min(width, 4 * LANES)
    sums = [jnp.zeros((8, chunk), jnp.float32)] * len(pairs)
    slots = []
    for pair in pairs:
        slots += [slot for slot in pair if not any(slot is known for known in slots)]
    places = [tuple(next(i for i, known in enumerate(slots) if known is slot) for slot in pair) for pair in pairs]
    for part in range(width // chunk):
        columns = slice(part * chunk, (part + 1) * chunk)

        def add_rows(index, sums, columns=columns):
            top = pl.multiple_of(index * 8, 8)
            tiles = [gradient_ref[slot, pl.ds(top, 8), columns] for slot in slots]
            return [total + tiles[a] * tiles[b] for total, (a, b) in zip(sums, places)]

        sums = lax.fori_loop(0, height // 8, add_rows, sums)
    rows = []
    for total in sums:
        row = sum(total[:, lane : lane + LANES] for lane in range(0, chunk, LANES))
        rows.append(jnp.sum(row, axis=0, keepdims=True))
    return rows


def store_inner(gram_ref, position, replicas, former, latter, row):
    row_former = (position[0] + replicas - former) % replicas
    row_latter = (position[0] + replicas - latter) % replicas
    gram_ref[pl.ds(row_former * replicas + row_latter, 1), :] = row
    gram_ref[pl.ds(row_latter * replicas + row_former, 1), :] = row


def early_kernel(replicas, scale_in, scale_out, position, own_ref, peer_ref, wide_own_ref, hidden_own_ref, *refs):
    hops = replicas - 2
    wide_right, wide_left, hidden_right, hidden_left = (refs[k * hops : (k + 1) * hops] for k in range(4))
    gram_ref, wide_ref, narrow_ref = refs[4 * hops :]
    quarter = own_ref.shape[1] // 2
    me = position[0]

    def gradient(slot, rows, wide_factor, hidden_factor):
        wide_ref[slot] = contract(rows[:, :quarter], wide_factor, 0, 0) * scale_in
        narrow_ref[slot] = contract(hidden_factor, rows[:, quarter:], 0, 0) * scale_out

    gradient(0, own_ref[...], wide_own_ref[...], hidden_own_ref[...])
    for slot in range(1, replicas):
        from_left = me >= slot
        late = (me == 0) if slot == 1 else (me == replicas - 1) if slot == replicas - 1 else me < 0
        if slot <= hops:
            @pl.when(from_left)
            def came_right(slot=slot):
                rows = slot_slice(peer_ref, slot - 1, 0, 2 * quarter)
                gradient(slot, rows, wide_right[slot - 1][...], hidden_right[slot - 1][...])

        if replicas - slot <= hops:
            @pl.when(jnp.logical_not(from_left))
            def came_left(slot=slot):
                rows = slot_slice(peer_ref, slot - 1, 0, 2 * quarter)
                hop = replicas - slot
                gradient(slot, rows, wide_left[hop - 1][...], hidden_left[hop - 1][...])

        @pl.when(late)
        def not_yet(slot=slot):
            wide_ref[slot] = jnp.zeros(wide_ref.shape[1:], jnp.float32)
            narrow_ref[slot] = jnp.zeros(narrow_ref.shape[1:], jnp.float32)

    pairs = replica_pairs(replicas)
    for pair, wide_row, narrow_row in zip(pairs, inner_rows(wide_ref, pairs), inner_rows(narrow_ref, pairs)):
        store_inner(gram_ref, position, replicas, *pair, wide_row + narrow_row)


def late_kernel(replicas, scale_in, scale_out, position, gram_in_ref, wide_in_ref, narrow_in_ref, peer_ref, *refs):
    wide_right, wide_left, hidden_right, hidden_left, gram_ref, wide_ref, narrow_ref = refs
    quarter = peer_ref.shape[3] // 2
    me = position[0]
    gram_ref[...] = gram_in_ref[...]

    def last(slot, wide_factor_ref, hidden_factor_ref):
        rows = slot_slice(peer_ref, slot - 1, 0, 2 * quarter)
        wide_ref[slot] = contract(rows[:, :quarter], wide_factor_ref[...], 0, 0) * scale_in
        narrow_ref[slot] = contract(hidden_factor_ref[...], rows[:, quarter:], 0, 0) * scale_out
        pairs = [(slot, other) for other in range(replicas)]
        for pair, wide_row, narrow_row in zip(pairs, inner_rows(wide_ref, pairs), inner_rows(narrow_ref, pairs)):
            store_inner(gram_ref, position, replicas, *pair, wide_row + narrow_row)

    @pl.when(me == 0)
    def left_end():
        last(1, wide_left, hidden_left)

    @pl.when(me == replicas - 1)
    def right_end():
        last(replicas - 1, wide_right, hidden_right)


def gradients(position, own, peers, wide_grad, hidden_act, wide_moves, hidden_moves, scale_in, scale_out):
    replicas = lax.axis_size("dp")
    quarter = own.shape[1] // 2
    early = [*wide_moves[0][:-1], *wide_moves[1][:-1], *hidden_moves[0][:-1], *hidden_moves[1][:-1]]
    late = [wide_moves[0][-1], wide_moves[1][-1], hidden_moves[0][-1], hidden_moves[1][-1]]
    outputs = [
        pltpu.VMEM((replicas * replicas, LANES), jnp.float32),
        pltpu.VMEM((replicas, quarter, wide_grad.shape[1]), jnp.float32),
        pltpu.VMEM((replicas, hidden_act.shape[1], quarter), jnp.float32),
    ]
    partial = pl.pallas_call(
        functools.partial(early_kernel, replicas, scale_in, scale_out),
        in_specs=[smem_spec()] + [vmem_spec()] * (4 + len(early)),
        out_specs=[vmem_spec()] * 3,
        out_shape=outputs,
        compiler_params=pltpu.CompilerParams(vmem_limit_bytes=24 * 1024 * 1024),
        name="early_gradients",
    )(position, own, peers, wide_grad, hidden_act, *early)
    return pl.pallas_call(
        functools.partial(late_kernel, replicas, scale_in, scale_out),
        in_specs=[smem_spec()] + [vmem_spec()] * (4 + len(late)),
        out_specs=[vmem_spec()] * 3,
        out_shape=outputs,
        input_output_aliases={2: 1, 3: 2},
        compiler_params=pltpu.CompilerParams(vmem_limit_bytes=24 * 1024 * 1024),
        name="late_gradients",
    )(position, *partial, peers, *late)


def assemble_kernel(replicas, hops, fresh, position, *refs):
    count = (1 if fresh else 0) + 2 * len(hops)
    narrow_refs, wide_refs = refs[:count], refs[count : 2 * count]
    narrow_out_ref, wide_out_ref, semaphores = refs[-3:]
    quarter = wide_refs[0].shape[1]
    me = position[0]
    moves = [(0, me >= 0)] if fresh else []
    for hop in hops:
        moves += [(-hop, me >= hop), (hop, me + hop < replicas)]

    def stores(index, shift):
        start = pl.multiple_of((me + shift) * quarter, quarter)
        return (
            pltpu.make_async_copy(
                narrow_refs[index], narrow_out_ref.at[:, :, pl.ds(start, quarter)], semaphores.at[0, index]
            ),
            pltpu.make_async_copy(
                wide_refs[index], wide_out_ref.at[0, :, pl.ds(start, quarter), :], semaphores.at[1, index]
            ),
        )

    for action in ("start", "wait"):
        for index, (shift, present) in enumerate(moves):
            @pl.when(present)
            def act(index=index, shift=shift, action=action):
                for store in stores(index, shift):
                    getattr(store, action)()


def assemble(position, replicas, hops, narrows, wides, narrow_shape, wide_shape, bases):
    fresh = not bases
    inputs = [*narrows, *wides, *bases]
    first_base = 1 + len(narrows) + len(wides)
    return pl.pallas_call(
        functools.partial(assemble_kernel, replicas, hops, fresh),
        in_specs=[smem_spec()] + [vmem_spec()] * (len(narrows) + len(wides)) + [hbm_spec()] * len(bases),
        out_specs=[hbm_spec()] * 2,
        out_shape=[
            jax.ShapeDtypeStruct(narrow_shape, jnp.bfloat16),
            jax.ShapeDtypeStruct(wide_shape, jnp.bfloat16),
        ],
        input_output_aliases={} if fresh else {first_base: 0, first_base + 1: 1},
        scratch_shapes=[pltpu.SemaphoreType.DMA((2, len(narrows)))],
        name="assemble_first" if fresh else "assemble_last",
    )(position, *inputs)


def tree_weights(gram, replicas):
    inner = [[gram[a * replicas + b : a * replicas + b + 1, :] for b in range(replicas)] for a in range(replicas)]
    weights = [{replica: None} for replica in range(replicas)]
    stride = replicas // 2
    while stride:
        for lower in range(stride):
            cross = inner[lower][lower + stride]
            norm_former = jnp.maximum(inner[lower][lower], 0.0)
            norm_latter = jnp.maximum(inner[lower + stride][lower + stride], 0.0)
            bound = jnp.sqrt(norm_former) * jnp.sqrt(norm_latter)
            cross = jnp.clip(cross, -bound, bound)
            former = 1.0 - cross / (2.0 * (norm_former + adasum_eps))
            latter = 1.0 - cross / (2.0 * (norm_latter + adasum_eps))
            joined = {}
            for side, factor in ((lower, former), (lower + stride, latter)):
                for replica, weight in weights[side].items():
                    joined[replica] = factor if weight is None else factor * weight
            weights[lower] = joined
            rows = [former * inner[lower][b] + latter * inner[lower + stride][b] for b in range(2 * stride)]
            inner[lower] = rows
            for a in range(2 * stride):
                if a != lower:
                    inner[a][lower] = former * inner[a][lower] + latter * inner[a][lower + stride]
            inner[lower][lower] = former * rows[lower] + latter * rows[lower + stride]
        stride //= 2
    return [weights[0][replica] for replica in range(replicas)]


def step_kernel(replicas, position, *refs):
    gram_refs = refs[:replicas]
    gradient_ref, momentum_ref, weight_ref, momentum_out_ref, weight_out_ref, mix_ref = refs[replicas:]
    total = gram_refs[0][...]
    for gram_ref in gram_refs[1:]:
        total = total + gram_ref[...]
    total = jnp.sum(total, axis=1, keepdims=True)
    total = jnp.broadcast_to(total, (total.shape[0], LANES))
    for replica, weight in enumerate(tree_weights(total, replicas)):
        mix_ref[replica : replica + 1, :] = weight
    parts, height, width = momentum_ref.shape
    step = 16
    weights = []
    for slot in range(replicas):
        row = mix_ref[pl.ds((position[0] + replicas - slot) % replicas, 1), :]
        weights.append(jnp.broadcast_to(jnp.concatenate([row] * (width // LANES), axis=1), (step, width)))
    for part in range(parts):
        columns = slice(part * width, (part + 1) * width)

        def update_rows(index, carry, part=part, columns=columns):
            rows = pl.ds(pl.multiple_of(index * step, step), step)
            momentum_new = momentum_coef * momentum_ref[part, rows, :]
            for slot in range(replicas):
                momentum_new = momentum_new + weights[slot] * gradient_ref[slot, rows, columns]
            momentum_out_ref[part, rows, :] = momentum_new
            weight = weight_ref[part, rows, :].astype(jnp.float32)
            weight_out_ref[part, rows, :] = (weight - learn_rate * momentum_new).astype(jnp.bfloat16)
            return carry

        lax.fori_loop(0, height // step, update_rows, 0)


def update(position, grams, gradient, momentum, weight):
    replicas = len(grams)
    return pl.pallas_call(
        functools.partial(step_kernel, replicas),
        in_specs=[smem_spec()] + [vmem_spec()] * (replicas + 3),
        out_specs=[vmem_spec()] * 2,
        out_shape=[
            jax.ShapeDtypeStruct(momentum.shape, jnp.float32),
            pltpu.VMEM(weight.shape, jnp.bfloat16),
        ],
        scratch_shapes=[pltpu.VMEM((8, LANES), jnp.float32)],
        compiler_params=pltpu.CompilerParams(vmem_limit_bytes=24 * 1024 * 1024),
    )(position, *grams, gradient, momentum, weight)


def relay(value):
    replicas = lax.axis_size("dp")
    rightward, leftward = [], []
    right, left = value, value
    for hop in range(1, replicas):
        right = lax.ppermute(right, "dp", [(i, i + 1) for i in range(hop - 1, replicas - 1)])
        left = lax.ppermute(left, "dp", [(i, i - 1) for i in range(1, replicas - hop + 1)])
        rightward.append(right)
        leftward.append(left)
    return rightward, leftward


def shards(
    tokens, cotangent, slot_rows, slot_count, slot_weight, w_in, w_out, momentum_in, momentum_out
):
    expert_axis = lax.axis_size("expert")
    replicas = lax.axis_size("dp")
    position = lax.axis_index("dp")
    position_arg = position.astype(jnp.int32).reshape(1)
    token_count, model_width = tokens.shape[1:]
    capacity = slot_rows.shape[-1]
    hidden = w_out.shape[1]
    quarter = model_width // replicas
    rows = expert_axis * capacity
    scale_in = model_width ** (-0.5)
    scale_out = hidden ** (-0.5)

    sent, *slices = dispatch(
        position_arg, slot_rows[0, 0], slot_count[0], slot_weight[0, 0], tokens[0], cotangent[0], replicas
    )
    moved = []
    for hop, piece in enumerate(slices, start=1):
        moved.append(lax.ppermute(piece, "dp", [(i, (i + hop) % replicas) for i in range(replicas)]))
    routed = lax.all_to_all(
        sent.reshape(expert_axis, capacity, 2 * model_width), "expert", split_axis=0, concat_axis=0, tiled=True
    ).reshape(rows, 2 * model_width)
    routed_rows = routed[:, :model_width]
    routed_cotan = routed[:, model_width:]

    gate_proj = jnp.dot(routed_rows, w_in[0, 0], preferred_element_type=jnp.float32) * scale_in
    up_proj = jnp.dot(routed_rows, w_in[0, 1], preferred_element_type=jnp.float32) * scale_in
    sigmoid_gate = jax.nn.sigmoid(gate_proj)
    activated = gate_proj * sigmoid_gate
    hidden_act = (activated * up_proj).astype(jnp.bfloat16)
    hidden_grad = contract(routed_cotan, w_out[0], 1, 1) * scale_out
    gate_grad = (
        hidden_grad * up_proj * sigmoid_gate * (1.0 + gate_proj * (1.0 - sigmoid_gate))
    ).astype(jnp.bfloat16)
    up_grad = (hidden_grad * activated).astype(jnp.bfloat16)
    wide_grad = jnp.concatenate([gate_grad, up_grad], axis=1)

    wide_moves = relay(wide_grad)
    hidden_moves = relay(hidden_act)
    own = jnp.concatenate(
        [
            lax.dynamic_slice_in_dim(routed, position * quarter, quarter, 1),
            lax.dynamic_slice_in_dim(routed, model_width + position * quarter, quarter, 1),
        ],
        axis=1,
    )
    peers = lax.all_to_all(
        jnp.stack([piece.reshape(expert_axis, capacity, 2 * quarter) for piece in moved], axis=1),
        "expert",
        split_axis=0,
        concat_axis=0,
        tiled=True,
    )

    rows_back = (
        (contract(gate_grad, w_in[0, 0], 1, 1) + contract(up_grad, w_in[0, 1], 1, 1)) * scale_in
    ).astype(jnp.bfloat16)
    returned = lax.all_to_all(
        rows_back.reshape(expert_axis, capacity, model_width), "expert", split_axis=0, concat_axis=0, tiled=True
    )
    flat_index = slot_rows.reshape(-1)
    one_hot = (
        flat_index[None, :] == lax.broadcasted_iota(jnp.int32, (token_count, flat_index.shape[0]), 0)
    ).astype(jnp.bfloat16)
    token_grad = jnp.dot(
        one_hot, returned.reshape(-1, model_width), preferred_element_type=jnp.float32
    ).astype(jnp.bfloat16)[None]

    wide_slice = lax.dynamic_slice_in_dim(w_in[0], position * quarter, quarter, 1)
    narrow_slice = lax.dynamic_slice_in_dim(w_out, position * quarter, quarter, 2)
    gram, gradient_wide, gradient_narrow = gradients(
        position_arg, own, peers, wide_grad, hidden_act, wide_moves, hidden_moves, scale_in, scale_out
    )
    grams = [gram]
    for hop in range(1, replicas):
        grams.append(lax.ppermute(gram, "dp", [(i, (i + hop) % replicas) for i in range(replicas)]))
    momentum_narrow, block_narrow = update(position_arg, grams, gradient_narrow, momentum_out, narrow_slice)
    momentum_wide, block_wide = update(position_arg, grams, gradient_wide, momentum_in[0], wide_slice)
    momentum_wide = momentum_wide[None]
    narrow_right, narrow_left = relay(block_narrow)
    wide_right, wide_left = relay(block_wide)
    early = tuple(range(1, replicas - 1))
    narrows = [block_narrow] + [move for hop in early for move in (narrow_right[hop - 1], narrow_left[hop - 1])]
    wide_parts = [block_wide] + [move for hop in early for move in (wide_right[hop - 1], wide_left[hop - 1])]
    bases = assemble(position_arg, replicas, early, narrows, wide_parts, w_out.shape, w_in.shape, ())
    new_narrow, new_wide = assemble(
        position_arg,
        replicas,
        (replicas - 1,),
        [narrow_right[-1], narrow_left[-1]],
        [wide_right[-1], wide_left[-1]],
        w_out.shape,
        w_in.shape,
        bases,
    )
    return (token_grad, new_wide, new_narrow, momentum_wide, momentum_narrow)


def solution(mesh):
    return sharded(shards, mesh)


def sharded(step, mesh):
    return jax.shard_map(
        step,
        mesh=mesh,
        in_specs=(
            P("dp", "expert", None),
            P("dp", "expert", None),
            P("dp", "expert", None, None),
            P("dp", "expert", None),
            P("dp", "expert", None, None),
            P("expert", None, None, None),
            P("expert", None, None),
            P("expert", None, "dp", None),
            P("expert", None, "dp"),
        ),
        out_specs=(
            P("dp", "expert", None),
            P("expert", None, None, None),
            P("expert", None, None),
            P("expert", None, "dp", None),
            P("expert", None, "dp"),
        ),
        check_vma=False,
    )
```
